32 devices in a mesh: seq: 4 (over y, core), wt: 8 (over z, x).
Axes of the slice: x: 2, y: 2, z: 4, core: 2. Of those that a mesh axis runs over, the one named last changes fastest.
Arguments:
- tokens: bfloat16 [8, 1024, 512], P('wt', 'seq'), may hold values from -6 to 6
- halted: int32 [8, 1024], P('wt', 'seq'), may hold values 0 or 1
- attn_ids: int32 [8, 1024, 4], P('wt', 'seq'), may hold values from 0 to 11, all different within a row
- ffn_ids: int32 [8, 1024, 2], P('wt', 'seq'), may hold values from 0 to 31, all different within a row; in each aligned block of 256 rows (0 to 255, 256 to 511, ..., all dimensions but the last counted through in order) at most 24 rows name the same one
- norm1: bfloat16 [512], P('wt'), may hold values from 0.25 to 1.75
- attn_router: bfloat16 [512, 12], P('wt'), may hold values from -0.13183594 to 0.13183594
- attn_kv: bfloat16 [512, 1024], P('wt'), may hold values from -0.25 to 0.25
- attn_query: bfloat16 [12, 512, 512], P(None, 'wt'), may hold values from -0.25 to 0.25
- attn_out: bfloat16 [12, 512, 512], P(None, 'wt'), may hold values from -8.4375 to 8.4375
- norm2: bfloat16 [512], P('wt'), may hold values from 0.25 to 1.75
- ffn_router: bfloat16 [512, 32], P('wt'), may hold values from -0.19824219 to 0.19824219
- ffn_in: bfloat16 [32, 512, 2048], P('wt'), may hold values from -0.25 to 0.25
- ffn_out: bfloat16 [32, 2048, 512], P('wt'), may hold values from -0.26367188 to 0.26367188
- halt_weight: bfloat16 [512], P('wt'), may hold values from -0.25 to 0.25
- cotangent: bfloat16 [8, 1024, 512], P('wt', 'seq'), may hold values from -6 to 6
Outputs:
- block_out: bfloat16 [8, 1024, 512], P('wt', 'seq')
- grad_tokens: float32 [8, 1024, 512], P('wt', 'seq')
- grad_norm1: float32 [512], P('wt')
- grad_attn_router: float32 [512, 12], P('wt')
- grad_attn_kv: float32 [512, 1024], P('wt')
- grad_attn_query: float32 [12, 512, 512], P(None, 'wt')
- grad_attn_out: float32 [12, 512, 512], P(None, 'wt')
- grad_norm2: float32 [512], P('wt')
- grad_ffn_router: float32 [512, 32], P('wt')
- grad_ffn_in: float32 [32, 512, 2048], P('wt')
- grad_ffn_out: float32 [32, 2048, 512], P('wt')
- grad_halt: float32 [512], P('wt')
The draws below stay inside these ranges and needn't reach their ends.
Inputs may be any that keep to these rules, and one draw needn't show every extreme that they name: `attn_ids`: each position names 4 different attention experts. `ffn_ids`: each position names 2 different feed-forward experts; within one sequence's aligned block of 256 positions no expert is named more than 24 times, and some block reaches 24.
All inputs are finite; a program needn't handle non-finite values. No bound on the sum of `halted` on one device may be relied on, other than what follows from the above.
Results may differ from the reference program's by a relative error of at most 0.02.
Values may be sent and summed in bfloat16 or wider, within the bound.
A program may use at most 256 MiB of HBM per device.

```python
import math
import jax
import jax.numpy as jnp
import numpy as np
from jax import lax

D = 512
H = 8
HD = 64
FE = 2048
EA = 12
EF = 32
KA = 4
KF = 2
BLOCK = 256
CAP = 24
SEQ_DEV = 256
LEN = 1024
NSEQ = 8


def touch_ends(array, rng, smallest, high):
    longest = array.shape.index(max(array.shape))
    spots = []
    for shift in (0, 1):
        where = [jax.random.randint(jax.random.fold_in(rng, axis), (), 0, length) for axis, length in enumerate(array.shape)]
        where[longest] = (where[longest] + shift) % array.shape[longest]
        spots.append(tuple(where))
    return array.at[spots[0]].set(smallest).at[spots[1]].set(high)


def steps_of(stream_key, dims, split, least, largest):
    level = 1.0
    for dim, parts in split:
        heights = jax.random.uniform(jax.random.fold_in(jax.random.fold_in(stream_key, 6), dim), (parts,), jnp.float32, least / len(split), largest / len(split))
        level = level * jnp.repeat(jnp.exp(heights), dims[dim] // parts).reshape((-1,) + (1,) * (len(dims) - 1 - dim))
    return level


def choose_distinct(rng, rows, count, top, lift):
    order = jax.random.permutation(jax.random.fold_in(rng, 1), count)
    boost = order
    for power in range(3):
        boost = boost * boost // count
    boost = boost * lift // count
    tickets = jax.random.randint(jax.random.fold_in(rng, 2), (rows, count), 0, 4096) + boost
    fixed_rows = jax.random.permutation(jax.random.fold_in(rng, 3), rows)[jnp.arange(count) % rows]
    tickets = jnp.where(jnp.arange(rows)[:, None] == fixed_rows[None, :], 1 << 14, tickets)
    score = tickets * count + jnp.arange(count)
    return lax.top_k(score.astype(jnp.int32), top)[1].astype(jnp.int32)


def shared_out(own_key, own, number, rows, count, top, most, slope):
    ranking = jax.random.permutation(own_key, count)
    crowded, usual = portions_of(count, rows * top, most, slope, True), portions_of(count, rows * top, most, slope, False)
    places = jnp.arange(count)

    def named(sizes, rotation):
        used = int((sizes > 0).sum())
        fixed = max(1, used // 4)
        moved = fixed + (places - fixed + rotation * (used - fixed)) % max(1, count - fixed)
        return jnp.zeros((count,), jnp.int32).at[ranking[jnp.where(places < fixed, places, moved)]].set(jnp.asarray(sizes, jnp.int32))

    sizes = jnp.where(number % 4 == 0, named(crowded, number // 4), named(usual, number - number // 4 - 1))
    mixed = jax.random.permutation(jax.random.fold_in(own, 3), count)
    source_of, receiver = mixed[0:count // 2 * 2:2], mixed[1:count // 2 * 2:2]
    room = jnp.minimum(sizes[source_of] - 1, most - sizes[receiver]) // 2
    room = jnp.where((source_of == ranking[0]) | (receiver == ranking[0]) | (sizes[receiver] == 0), 0, jnp.maximum(room, 0))
    moved = jax.random.randint(jax.random.fold_in(own, 4), (count // 2,), 0, 1 << 20) % (room + 1)
    sizes = sizes.at[source_of].add(-moved).at[receiver].add(moved)
    labels = jnp.searchsorted(jnp.cumsum(sizes), jnp.arange(rows * top), side="right").astype(jnp.int32)
    grid = labels.reshape(top, rows).T
    grid = grid[jax.random.permutation(jax.random.fold_in(own, 1), rows)]
    rotation = jax.random.randint(jax.random.fold_in(own, 2), (rows, 1), 0, top)
    return jnp.take_along_axis(grid, (jnp.arange(top)[None, :] + rotation) % top, axis=1)


def portions_of(number_of, total, bound, skew, full):
    weights = [(1 << 20) // math.isqrt(rank ** skew) + 1 for rank in range(1, number_of + 1)]
    largest = bound if full else min(bound, max(-(-total // number_of), total * weights[0] // sum(weights)))
    least = 1 if total - largest >= number_of - 1 else 0
    given, rest = [largest] + [least] * (number_of - 1), total - largest - least * (number_of - 1)
    while rest > 0:
        movable = [i for i in range(1, number_of) if given[i] < largest] or [i for i in range(1, number_of) if given[i] < bound]
        pool, remaining = sum([weights[i] for i in movable]), rest
        for i in movable:
            more = min(bound - given[i], max(1, remaining * weights[i] // pool), rest)
            given[i] = given[i] + more
            rest = rest - more
    return np.array(given)


def gaussian(own_key, extent, deviation, bound, cuts=(), held_as=jnp.bfloat16):
    result = deviation * jax.random.normal(own_key, extent, jnp.float32)
    if cuts:
        result = result * steps_of(own_key, extent, cuts, -0.22, 0.18)
    return jnp.clip(result, -bound, bound).astype(held_as)


def setup_inputs(seed: int = 0) -> dict:
    key_list = jax.random.split(jax.random.key(seed), 16)
    tokens = gaussian(key_list[0], (NSEQ, LEN, D), 1.0, 6.0, ((0, 8), (1, 4)))
    halted = touch_ends((jax.random.randint(key_list[1], (NSEQ, LEN), 0, 4) < 1).astype(jnp.int32), jax.random.fold_in(key_list[1], 1), 0, 1)
    attn_ids = choose_distinct(key_list[2], NSEQ * LEN, EA, KA, 2730).reshape((NSEQ, LEN, KA))
    ffn_ids_keys = jax.random.split(jax.random.fold_in(key_list[3], 1), NSEQ * LEN // SEQ_DEV)
    ffn_ids_turns = jax.random.permutation(jax.random.fold_in(key_list[3], 3), NSEQ * LEN // SEQ_DEV)
    ffn_ids = jax.vmap(lambda own, number: shared_out(jax.random.fold_in(key_list[3], 2), own, number, SEQ_DEV, EF, KF, CAP, 1))(ffn_ids_keys, ffn_ids_turns).reshape((NSEQ, LEN, KF))
    norm1 = jnp.clip(1.0 + 0.15 * jax.random.normal(key_list[4], (D,), jnp.float32), 0.25, 1.75).astype(jnp.bfloat16)
    attn_router = gaussian(key_list[5], (D, EA), (0.5 * D ** -0.5), 0.13183594, ((0, 8),))
    attn_kv = gaussian(key_list[6], (D, 2 * D), D ** -0.5, 0.25, ((0, 8),))
    attn_query = gaussian(key_list[7], (EA, D, D), D ** -0.5, 0.25, ((1, 8),))
    attn_out = gaussian(key_list[8], (EA, D, D), (32 * D ** -0.5), 8.4375, ((1, 8),))
    norm2 = jnp.clip(1.0 + 0.15 * jax.random.normal(key_list[9], (D,), jnp.float32), 0.25, 1.75).astype(jnp.bfloat16)
    ffn_router = gaussian(key_list[10], (D, EF), (0.75 * D ** -0.5), 0.19824219, ((0, 8),))
    ffn_in = gaussian(key_list[11], (EF, D, FE), D ** -0.5, 0.25, ((0, 8),))
    ffn_out = gaussian(key_list[12], (EF, FE, D), (2 * FE ** -0.5), 0.26367188, ((0, 8),))
    halt_weight = gaussian(key_list[13], (D,), D ** -0.5, 0.25, ((0, 8),))
    cotangent = gaussian(key_list[14], (NSEQ, LEN, D), 1.0, 6.0, ((0, 8), (1, 4)))
    return dict(tokens=tokens, halted=halted, attn_ids=attn_ids, ffn_ids=ffn_ids, norm1=norm1, attn_router=attn_router, attn_kv=attn_kv, attn_query=attn_query, attn_out=attn_out, norm2=norm2, ffn_router=ffn_router, ffn_in=ffn_in, ffn_out=ffn_out, halt_weight=halt_weight, cotangent=cotangent)


@jax.custom_vjp
def low(v):
    return lax.optimization_barrier(v.astype(jnp.bfloat16)).astype(jnp.float32)

@jax.custom_vjp
def low_back(v):
    return v

def low_keep(v):
    return (low(v), None)

def low_pass(kept, grad):
    return (grad,)

def back_keep(v):
    return (v, None)

def back_low(kept, grad):
    return (low(grad),)
low.defvjp(low_keep, low_pass)
low_back.defvjp(back_keep, back_low)
norm_epsilon = 1e-05

def layer_norm(stream, gain):
    center = lax.optimization_barrier(jnp.mean(stream, -1, keepdims=True))
    shifted = stream - center
    return shifted * lax.rsqrt(lax.optimization_barrier(jnp.mean(shifted * shifted, -1, keepdims=True)) + norm_epsilon) * gain

def pick_gates(logits, onehot):
    picked = jnp.einsum('lke,le->lk', onehot, logits, precision=lax.Precision.HIGHEST)
    return jax.nn.softmax(picked, -1)

def slot_places(pick):
    block_count = pick.shape[0]
    flattened = pick.reshape(block_count, -1)
    member = (flattened[:, :, None] == jnp.arange(EF, dtype=jnp.int32)).astype(jnp.int32)
    earlier = jnp.cumsum(member, 1) - member
    return (flattened * CAP + lax.optimization_barrier(jnp.sum(earlier * member, -1))).astype(jnp.int32).reshape(pick.shape)

def attend(queries, key_rows, value_rows):

    def one_block(offset):
        query_block = lax.dynamic_slice_in_dim(queries, offset, BLOCK, 0)
        scores = jnp.einsum('bkhd,jhd->hbkj', query_block, key_rows, precision=lax.Precision.HIGHEST) * HD ** (-0.5)
        allowed = jnp.arange(LEN, dtype=jnp.int32) < offset + BLOCK
        scores = low_back(jnp.where(allowed, scores, -1e+30))
        log_total = jax.nn.logsumexp(scores, -1, keepdims=True)
        weights_low = low(jnp.exp(scores - log_total))
        return jnp.einsum('hbkj,jhd->bkhd', weights_low, value_rows, precision=lax.Precision.HIGHEST)
    offsets = jnp.arange(LEN // BLOCK, dtype=jnp.int32) * BLOCK
    return lax.map(jax.checkpoint(one_block), offsets).reshape(LEN, KA, H, HD)

def sequence_forward(params, stream, live_rows, attn_pick, ffn_pick):
    gain_first, attn_route, key_value, query_proj, output_proj, gain_second, ffn_route, expand_proj, shrink_proj, halting = params
    attn_input = low(layer_norm(stream, gain_first))
    attn_logits = low_back(jnp.dot(attn_input, attn_route, precision=lax.Precision.HIGHEST))
    attn_hot = jax.nn.one_hot(attn_pick, EA, dtype=jnp.float32)
    attn_gates = pick_gates(attn_logits, attn_hot)
    pairs = low_back(low(jnp.dot(attn_input, key_value, precision=lax.Precision.HIGHEST))).reshape(LEN, H, 2 * HD)
    query_all = jnp.einsum('ld,edf->lef', attn_input, query_proj, precision=lax.Precision.HIGHEST)
    queries = jnp.einsum('lke,lef->lkf', attn_hot, query_all, precision=lax.Precision.HIGHEST)
    queries = low_back(low(queries)).reshape(LEN, KA, H, HD)
    mixture = attend(queries, pairs[:, :, :HD], pairs[:, :, HD:])
    mixture = low_back(low(mixture)).reshape(LEN, KA, D)
    mix_select = jnp.einsum('lke,lkf->lef', attn_hot, mixture, precision=lax.Precision.HIGHEST)
    branch = low_back(jnp.einsum('lef,efd->led', mix_select, output_proj, precision=lax.Precision.HIGHEST))
    attn_select = jnp.einsum('lke,lk->le', attn_hot, attn_gates, precision=lax.Precision.HIGHEST)
    after_attn = stream + jnp.einsum('le,led->ld', attn_select, branch, precision=lax.Precision.HIGHEST)
    ffn_input = low(layer_norm(after_attn, gain_second))
    ffn_logits = low_back(jnp.dot(ffn_input, ffn_route, precision=lax.Precision.HIGHEST))
    ffn_hot = jax.nn.one_hot(ffn_pick, EF, dtype=jnp.float32)
    ffn_gates = pick_gates(ffn_logits, ffn_hot)
    block_count = LEN // SEQ_DEV
    places = slot_places(ffn_pick.reshape(block_count, SEQ_DEV, KF))
    place_hot = jax.nn.one_hot(places, EF * CAP, dtype=jnp.float32)
    input_blocks = ffn_input.reshape(block_count, SEQ_DEV, D)
    dispatch = jnp.einsum('bskc,bsd->bcd', place_hot, input_blocks, precision=lax.Precision.HIGHEST)
    dispatch = low_back(dispatch).reshape(block_count, EF, CAP, D)
    pre = low_back(jnp.einsum('becd,edf->becf', dispatch, expand_proj, precision=lax.Precision.HIGHEST))
    hidden = low(jax.nn.gelu(pre, approximate=True))
    slot_out = jnp.einsum('becf,efd->becd', hidden, shrink_proj, precision=lax.Precision.HIGHEST)
    slot_out = low_back(low(slot_out)).reshape(block_count, EF * CAP, D)
    expert_out = jnp.einsum('bskc,bcd->bskd', place_hot, slot_out, precision=lax.Precision.HIGHEST).reshape(LEN, KF, D)
    after_ffn = after_attn + jnp.einsum('lk,lkd->ld', ffn_gates, expert_out, precision=lax.Precision.HIGHEST)
    halt = jax.nn.sigmoid(lax.optimization_barrier(jnp.sum(after_ffn * halting, -1, keepdims=True)))
    return stream + live_rows * (1.0 - halt) * (after_ffn - stream)

def reference(tokens, halted, attn_ids, ffn_ids, norm1, attn_router, attn_kv, attn_query, attn_out, norm2, ffn_router, ffn_in, ffn_out, halt_weight, cotangent):
    weights = (norm1.astype(jnp.float32), attn_router.astype(jnp.float32), attn_kv.astype(jnp.float32), attn_query.astype(jnp.float32), attn_out.astype(jnp.float32), norm2.astype(jnp.float32), ffn_router.astype(jnp.float32), ffn_in.astype(jnp.float32), ffn_out.astype(jnp.float32), halt_weight.astype(jnp.float32))
    stream_in = tokens.astype(jnp.float32)
    live = (1 - halted).astype(jnp.float32)[:, :, None]

    def forward(stream, params):
        one_sequence = jax.checkpoint(sequence_forward)

        def scan_step(running, pieces):
            return (running, one_sequence(params, pieces[0], pieces[1], pieces[2], pieces[3]))
        finished, outputs = lax.scan(scan_step, jnp.zeros((), jnp.float32), (stream, live, attn_ids, ffn_ids))
        return outputs
    block_out, pullback = jax.vjp(forward, stream_in, weights)
    grad_tokens, grads = pullback(cotangent.astype(jnp.float32))
    return (block_out.astype(jnp.bfloat16), grad_tokens, grads[0], grads[1], grads[2], grads[3], grads[4], grads[5], grads[6], grads[7], grads[8], grads[9])
```

```python
import functools

import jax
import jax.numpy as jnp
from jax import lax
from jax.experimental import pallas as pl
from jax.experimental.pallas import tpu as pltpu
from jax.sharding import PartitionSpec as P

HD = 64
EA = 12
EF = 32
KA = 4
KF = 2
CAP = 24
EPS = 1e-05
BF = jnp.bfloat16
F32 = jnp.float32

C_N1, C_N2, C_HALT, C_AR, C_FR, C_END = 0, 1, 2, 3, 15, 47


def dot(a, b, ca=1, cb=0):
    return lax.dot_general(a, b, (((ca,), (cb,)), ((), ())), preferred_element_type=F32)


def layer_norm(stream):
    center = jnp.mean(stream, -1, keepdims=True)
    shifted = stream - center
    spread = lax.rsqrt(jnp.mean(shifted * shifted, -1, keepdims=True) + EPS)
    return shifted * spread, spread


def norm_back(grad_normed, normed, spread, gain):
    scaled = grad_normed * gain
    return spread * (
        scaled
        - jnp.mean(scaled, -1, keepdims=True)
        - normed * jnp.mean(scaled * normed, -1, keepdims=True)
    )


def gelu_parts(v):
    c0, c1 = 0.7978845608028654, 0.044715
    v2 = v * v
    t = jnp.tanh(c0 * (v + c1 * (v2 * v)))
    half = 0.5 * (1.0 + t)
    value = v * half
    slope = half + 0.5 * v * (1.0 - t * t) * (c0 * (1.0 + 3.0 * c1 * v2))
    return value, slope


def vmem():
    return pl.BlockSpec(memory_space=pltpu.VMEM)


def attn_fwd_kernel(
    nb, hd, x_ref, ids_ref, small_ref, wq_ref, wkv_ref, wout_ref,
    part_ref, q_ref, kv_ref, mix_ref, gate_ref,
    kv_scr, qa_scr, a_scr,
):
    T = x_ref.shape[0]
    C = hd * HD
    b = pl.program_id(0)
    xb = x_ref[...]
    ids = ids_ref[...]
    kvb = dot(xb, wkv_ref[...]).astype(BF)
    kv_ref[...] = kvb
    kv_scr[pl.ds(pl.multiple_of(b * T, T), T), :] = kvb
    logits = dot(xb, small_ref[...])
    lane = lax.broadcasted_iota(jnp.int32, logits.shape, 1)
    picked = [
        jnp.sum(jnp.where(lane == ids[:, k : k + 1] + C_AR, logits, 0.0), -1, keepdims=True)
        for k in range(KA)
    ]
    top = functools.reduce(jnp.maximum, picked)
    ex = [jnp.exp(p - top) for p in picked]
    tot = functools.reduce(jnp.add, ex)
    gates = [e / tot for e in ex]
    gate_ref[...] = jnp.concatenate(gates, 1)

    qa_scr[...] = dot(xb, wq_ref[...])
    for k in range(KA):
        idk = jnp.broadcast_to(ids[:, k : k + 1], (T, C))
        acc = jnp.zeros((T, C), F32)
        for e in range(EA):
            acc = jnp.where(idk == e, qa_scr[:, e * C : (e + 1) * C], acc)
        q_ref[k] = (acc * (HD**-0.5)).astype(BF)

    for blk in range(nb):

        @pl.when(b == blk)
        def _(blk=blk):
            seen = (blk + 1) * T
            for i in range(hd):
                keys = kv_scr[0:seen, i * 2 * HD : i * 2 * HD + HD]
                vals = kv_scr[0:seen, i * 2 * HD + HD : (i + 1) * 2 * HD]

                def body(k, carry):
                    qk = q_ref[k, :, i * HD : (i + 1) * HD]
                    s = dot(qk, keys, 1, 1)
                    m = jnp.max(s, -1, keepdims=True)
                    p = jnp.exp(s - m)
                    l = jnp.sum(p, -1, keepdims=True)
                    o = dot(p.astype(BF), vals) / l
                    mix_ref[k, :, i * HD : (i + 1) * HD] = o.astype(BF)
                    return carry

                lax.fori_loop(0, KA, body, 0, unroll=2)

    scatter_pairs(ids, [gates[k] * mix_ref[k].astype(F32) for k in range(KA)], a_scr, C)
    part_ref[...] = dot(a_scr[...], wout_ref[...]).astype(part_ref.dtype)


def scatter_pairs(ids, rows, out_ref, C):
    T = ids.shape[0]
    idk = [jnp.broadcast_to(ids[:, k : k + 1], (T, C)) for k in range(KA)]
    for e in range(EA):
        acc = jnp.zeros((T, C), F32)
        for k in range(KA):
            acc = jnp.where(idk[k] == e, rows[k], acc)
        out_ref[:, e * C : (e + 1) * C] = acc.astype(BF)


def attn_forward(x_all, ids_all, small, wq, wkv, wout, T, hd):
    L, D = x_all.shape
    nb = L // T
    C = hd * HD
    return pl.pallas_call(
        functools.partial(attn_fwd_kernel, nb, hd),
        name="attn_forward",
        grid=(nb,),
        out_shape=(
            jax.ShapeDtypeStruct((L, D), BF),
            jax.ShapeDtypeStruct((KA, L, C), BF),
            jax.ShapeDtypeStruct((L, 2 * C), BF),
            jax.ShapeDtypeStruct((KA, L, C), BF),
            jax.ShapeDtypeStruct((L, KA), F32),
        ),
        in_specs=[
            pl.BlockSpec((T, D), lambda b: (b, 0)),
            pl.BlockSpec((T, KA), lambda b: (b, 0)),
            vmem(), vmem(), vmem(), vmem(),
        ],
        out_specs=(
            pl.BlockSpec((T, D), lambda b: (b, 0)),
            pl.BlockSpec((KA, T, C), lambda b: (0, b, 0)),
            pl.BlockSpec((T, 2 * C), lambda b: (b, 0)),
            pl.BlockSpec((KA, T, C), lambda b: (0, b, 0)),
            pl.BlockSpec((T, KA), lambda b: (b, 0)),
        ),
        scratch_shapes=[
            pltpu.VMEM((L, 2 * C), BF),
            pltpu.VMEM((T, EA * C), F32),
            pltpu.VMEM((T, EA * C), BF),
        ],
    )(x_all, ids_all, small, wq, wkv, wout)


def attn_bwd_kernel(
    nb, hd, x_ref, d_ref, ids_ref, gate_ref, q_ref, kv_ref, mix_ref, wq_ref, wkv_ref, wout_ref,
    dx_ref, dg_ref, gq_ref, gkv_ref, gout_ref,
    gq_scr, gkv_scr, gout_scr, dkv_scr, big_scr, a_scr, do_scr, dq_scr, pt_scr, ds_scr,
):
    T = x_ref.shape[0]
    C = hd * HD
    step = pl.program_id(0)
    b = nb - 1 - step

    @pl.when(step == 0)
    def _():
        gq_scr[...] = jnp.zeros_like(gq_scr)
        gkv_scr[...] = jnp.zeros_like(gkv_scr)
        gout_scr[...] = jnp.zeros_like(gout_scr)
        dkv_scr[...] = jnp.zeros_like(dkv_scr)

    xb = x_ref[...]
    db = d_ref[...]
    ids = ids_ref[...]
    gates = gate_ref[...]
    big_scr[...] = dot(db, wout_ref[...], 1, 1)
    dgs = []
    for k in range(KA):
        idk = jnp.broadcast_to(ids[:, k : k + 1], (T, C))
        acc = jnp.zeros((T, C), F32)
        for e in range(EA):
            acc = jnp.where(idk == e, big_scr[:, e * C : (e + 1) * C], acc)
        dgs.append(jnp.sum(acc * mix_ref[k].astype(F32), -1, keepdims=True))
        do_scr[k] = (acc * gates[:, k : k + 1]).astype(BF)
    dg_ref[...] = jnp.concatenate(dgs, 1)
    scatter_pairs(ids, [gates[:, k : k + 1] * mix_ref[k].astype(F32) for k in range(KA)], a_scr, C)
    gout_scr[...] += dot(a_scr[...], db, 0, 0)

    for blk in range(nb):

        @pl.when(b == blk)
        def _(blk=blk):
            seen = (blk + 1) * T
            for i in range(hd):
                lo, mid, hi = i * 2 * HD, i * 2 * HD + HD, (i + 1) * 2 * HD
                keys = kv_ref[0:seen, lo:mid]
                vals = kv_ref[0:seen, mid:hi]
                for k in range(KA):
                    qk = q_ref[k, :, i * HD : (i + 1) * HD]
                    dok = do_scr[k, :, i * HD : (i + 1) * HD]
                    s = dot(keys, qk, 1, 1)
                    m = jnp.max(s, 0, keepdims=True)
                    p = jnp.exp(s - m)
                    p = p * (1.0 / jnp.sum(p, 0, keepdims=True))
                    t = p * dot(vals, dok, 1, 1)
                    delta = jnp.sum(t, 0, keepdims=True)
                    ds = (t - p * delta).astype(BF)
                    pt_scr[0:seen, k * T : (k + 1) * T] = p.astype(BF)
                    ds_scr[0:seen, k * T : (k + 1) * T] = ds
                    dq_scr[k, :, i * HD : (i + 1) * HD] = (dot(ds, keys, 0, 0) * (HD**-0.5)).astype(BF)
                q_rows = q_ref[:, :, i * HD : (i + 1) * HD].reshape(KA * T, HD)
                do_rows = do_scr[:, :, i * HD : (i + 1) * HD].reshape(KA * T, HD)
                dkv_scr[0:seen, lo:mid] += dot(ds_scr[0:seen, :], q_rows)
                dkv_scr[0:seen, mid:hi] += dot(pt_scr[0:seen, :], do_rows)

    scatter_pairs(ids, [dq_scr[k].astype(F32) for k in range(KA)], a_scr, C)
    dkv = dkv_scr[pl.ds(pl.multiple_of(b * T, T), T), :].astype(BF)
    dx = dot(a_scr[...], wq_ref[...], 1, 1) + dot(dkv, wkv_ref[...], 1, 1)
    dx_ref[...] = dx.astype(dx_ref.dtype)
    gq_scr[...] += dot(xb, a_scr[...], 0, 0)
    gkv_scr[...] += dot(xb, dkv, 0, 0)

    @pl.when(step == nb - 1)
    def _():
        gq_ref[...] = gq_scr[...].astype(BF)
        gkv_ref[...] = gkv_scr[...].astype(BF)
        gout_ref[...] = gout_scr[...].astype(BF)


def attn_backward(x_all, d_all, ids_all, gates, q, kv, mix, wq, wkv, wout, T, hd):
    L, D = x_all.shape
    nb = L // T
    C = hd * HD
    return pl.pallas_call(
        functools.partial(attn_bwd_kernel, nb, hd),
        name="attn_backward",
        grid=(nb,),
        out_shape=(
            jax.ShapeDtypeStruct((L, D), BF),
            jax.ShapeDtypeStruct((L, KA), F32),
            jax.ShapeDtypeStruct((D, EA * C), BF),
            jax.ShapeDtypeStruct((D, 2 * C), BF),
            jax.ShapeDtypeStruct((EA * C, D), BF),
        ),
        in_specs=[
            pl.BlockSpec((T, D), lambda i: (nb - 1 - i, 0)),
            pl.BlockSpec((T, D), lambda i: (nb - 1 - i, 0)),
            pl.BlockSpec((T, KA), lambda i: (nb - 1 - i, 0)),
            pl.BlockSpec((T, KA), lambda i: (nb - 1 - i, 0)),
            pl.BlockSpec((KA, T, C), lambda i: (0, nb - 1 - i, 0)),
            vmem(),
            pl.BlockSpec((KA, T, C), lambda i: (0, nb - 1 - i, 0)),
            vmem(), vmem(), vmem(),
        ],
        out_specs=(
            pl.BlockSpec((T, D), lambda i: (nb - 1 - i, 0)),
            pl.BlockSpec((T, KA), lambda i: (nb - 1 - i, 0)),
            vmem(), vmem(), vmem(),
        ),
        scratch_shapes=[
            pltpu.VMEM((D, EA * C), F32),
            pltpu.VMEM((D, 2 * C), F32),
            pltpu.VMEM((EA * C, D), F32),
            pltpu.VMEM((L, 2 * C), F32),
            pltpu.VMEM((T, EA * C), F32),
            pltpu.VMEM((T, EA * C), BF),
            pltpu.VMEM((KA, T, C), BF),
            pltpu.VMEM((KA, T, C), BF),
            pltpu.VMEM((L, KA * T), BF),
            pltpu.VMEM((L, KA * T), BF),
        ],
    )(x_all, d_all, ids_all, gates, q, kv, mix, wq, wkv, wout)


def rows_of(ref):
    value = ref[...]
    return value.astype(F32).reshape(-1, value.shape[-1]).astype(BF)


def ffn_fwd_kernel(x_ref, w1_ref, w2_ref, out_ref):
    x = rows_of(x_ref)
    FE = w1_ref.shape[-1]
    step = 512
    acc = jnp.zeros((x.shape[0], x.shape[1]), F32)
    for c in range(0, FE, step):
        value, _ = gelu_parts(dot(x, w1_ref[0, :, c : c + step]))
        acc = acc + dot(value.astype(BF), w2_ref[0, c : c + step, :])
    out_ref[...] = acc.reshape(out_ref.shape).astype(BF)


def ffn_bwd_kernel(x_ref, dy_ref, w1_ref, w2_ref, out_ref):
    x = rows_of(x_ref)
    dy = rows_of(dy_ref)
    FE = w1_ref.shape[-1]
    step = 512
    acc = jnp.zeros((x.shape[0], x.shape[1]), F32)
    for c in range(0, FE, step):
        _, slope = gelu_parts(dot(x, w1_ref[0, :, c : c + step]))
        dpre = dot(dy, w2_ref[0, c : c + step, :], 1, 1) * slope
        acc = acc + dot(dpre.astype(BF), w1_ref[0, :, c : c + step], 1, 1)
    out_ref[...] = acc.reshape(out_ref.shape).astype(BF)


def ffn_grad_kernel(x_ref, dy_ref, w1_ref, w2_ref, g1_ref, g2_ref):
    x = rows_of(x_ref)
    dy = rows_of(dy_ref)

    @pl.when(pl.program_id(2) == 0)
    def _():
        g1_ref[...] = jnp.zeros_like(g1_ref)
        g2_ref[...] = jnp.zeros_like(g2_ref)

    value, slope = gelu_parts(dot(x, w1_ref[0]))
    dpre = (dot(dy, w2_ref[0], 1, 1) * slope).astype(BF)
    g1_ref[0] += dot(x, dpre, 0, 0)
    g2_ref[0] += dot(value.astype(BF), dy, 0, 0)


def ffn_specs(W, D, FE):
    return (
        pl.BlockSpec((W, 1, CAP, D), lambda j: (0, j, 0, 0)),
        pl.BlockSpec((1, D, FE), lambda j: (j, 0, 0)),
        pl.BlockSpec((1, FE, D), lambda j: (j, 0, 0)),
    )


def ffn_forward(x, w1, w2):
    W, EL, _, D = x.shape
    rows, one, two = ffn_specs(W, D, w1.shape[-1])
    return pl.pallas_call(
        ffn_fwd_kernel, name="ffn_forward", grid=(EL,),
        out_shape=jax.ShapeDtypeStruct(x.shape, BF),
        in_specs=[rows, one, two], out_specs=rows,
    )(x, w1, w2)


def ffn_backward(x, dy, w1, w2):
    W, EL, _, D = x.shape
    rows, one, two = ffn_specs(W, D, w1.shape[-1])
    return pl.pallas_call(
        ffn_bwd_kernel, name="ffn_backward", grid=(EL,),
        out_shape=jax.ShapeDtypeStruct(x.shape, BF),
        in_specs=[rows, rows, one, two], out_specs=rows,
    )(x, dy, w1, w2)


def ffn_grads(x, dy, w1, w2):
    S, W, EL, _, D = x.shape
    FE = w1.shape[-1]
    ns = max(1, min(S, 768 // (W * CAP)))
    chunk = 512
    rows = pl.BlockSpec((ns, W, 1, CAP, D), lambda j, c, r: (r, 0, j, 0, 0))
    one = pl.BlockSpec((1, D, chunk), lambda j, c, r: (j, 0, c))
    two = pl.BlockSpec((1, chunk, D), lambda j, c, r: (j, c, 0))
    return pl.pallas_call(
        ffn_grad_kernel, name="ffn_grads", grid=(EL, FE // chunk, S // ns),
        out_shape=(jax.ShapeDtypeStruct(w1.shape, F32), jax.ShapeDtypeStruct(w2.shape, F32)),
        in_specs=[rows, rows, one, two], out_specs=(one, two),
    )(x, dy, w1, w2)


def per_device(
    tokens, halted, attn_ids, ffn_ids, norm1, attn_router, attn_kv, attn_query, attn_out,
    norm2, ffn_router, ffn_in, ffn_out, halt_weight, cotangent,
):
    _, T, D = tokens.shape
    S, W = lax.axis_size("seq"), lax.axis_size("wt")
    s = lax.axis_index("seq")
    hd = D // HD // S
    C = hd * HD
    EL = ffn_in.shape[0]
    rows_w = norm1.shape[0]
    slots = EF * CAP

    tokens, halted, attn_ids, ffn_ids = tokens[0], halted[0], attn_ids[0], ffn_ids[0]
    cot = cotangent[0].astype(F32)
    stream = tokens.astype(F32)

    pack = jnp.concatenate(
        [norm1[:, None], norm2[:, None], halt_weight[:, None], attn_router, ffn_router,
         jnp.zeros((rows_w, 128 - C_END), BF)], 1)
    small = lax.all_gather(pack, "wt", axis=0, tiled=True)
    gain1 = small[:, C_N1].astype(F32)[None]
    gain2 = small[:, C_N2].astype(F32)[None]
    halting = small[:, C_HALT].astype(F32)[None]

    wq_mine = lax.dynamic_slice_in_dim(attn_query, s * C, C, 2).transpose(1, 0, 2).reshape(rows_w, EA * C)
    wkv_mine = lax.dynamic_slice_in_dim(attn_kv, s * 2 * C, 2 * C, 1)
    wq = lax.all_gather(wq_mine, "wt", axis=0, tiled=True)
    wkv = lax.all_gather(wkv_mine, "wt", axis=0, tiled=True)
    wo = lax.dynamic_slice_in_dim(attn_out, s * C, C, 2)
    wo = lax.all_gather(wo, "wt", axis=1, tiled=True)
    wout = lax.all_to_all(wo, "seq", split_axis=1, concat_axis=2, tiled=True).reshape(EA * C, D)

    normed1, spread1 = layer_norm(stream)
    attn_in = (normed1 * gain1).astype(BF)
    x_all = lax.all_gather(attn_in, "seq", axis=0, tiled=True)
    ids_all = lax.all_gather(attn_ids, "seq", axis=0, tiled=True)

    part, q, kv, mix, gates_all = attn_forward(x_all, ids_all, small, wq, wkv, wout, T, hd)
    parts = lax.all_to_all(part, "seq", split_axis=0, concat_axis=0, tiled=True).reshape(S, T, D)
    after_attn = stream + jnp.sum(parts.astype(F32), 0)

    normed2, spread2 = layer_norm(after_attn)
    ffn_x = (normed2 * gain2).astype(BF)
    logits = dot(ffn_x, small[:, C_FR:C_END])
    expert = jnp.arange(EF, dtype=jnp.int32)[None]
    hots = [(ffn_ids[:, k : k + 1] == expert).astype(F32) for k in range(KF)]
    picked = jnp.concatenate([jnp.sum(h * logits, -1, keepdims=True) for h in hots], 1)
    gates = jax.nn.softmax(picked, -1)
    before = (jnp.arange(T)[:, None] > jnp.arange(T)[None, :]).astype(BF)
    rank = dot(before, (hots[0] + hots[1]).astype(BF))
    places = [
        ffn_ids[:, k] * CAP + jnp.sum(hots[k] * rank, -1).astype(jnp.int32) for k in range(KF)
    ]
    slot = jnp.arange(slots, dtype=jnp.int32)[None]
    place_hot = [(p[:, None] == slot).astype(BF) for p in places]
    both_hot = place_hot[0] + place_hot[1]

    dispatch = dot(both_hot, ffn_x, 0, 0).astype(BF)
    received = lax.all_to_all(dispatch, "wt", split_axis=0, concat_axis=0, tiled=True)
    received = received.reshape(W, EL, CAP, D)
    slot_out = ffn_forward(received, ffn_in, ffn_out)
    returned = lax.all_to_all(slot_out.reshape(slots, D), "wt", split_axis=0, concat_axis=0, tiled=True)
    expert_rows = [dot(h, returned) for h in place_hot]
    after_ffn = after_attn + gates[:, 0:1] * expert_rows[0] + gates[:, 1:2] * expert_rows[1]
    live = (1 - halted).astype(F32)[:, None]
    halt = jax.nn.sigmoid(jnp.sum(after_ffn * halting, -1, keepdims=True))
    keep = live * (1.0 - halt)
    block_out = (stream + keep * (after_ffn - stream)).astype(BF)

    d_halt = -live * halt * (1.0 - halt) * jnp.sum((after_ffn - stream) * cot, -1, keepdims=True)
    g_halt = jnp.sum(d_halt * after_ffn, 0)
    d_after_ffn = keep * cot + d_halt * halting
    d_slots = sum(
        dot(place_hot[k], (gates[:, k : k + 1] * d_after_ffn).astype(BF), 0, 0) for k in range(KF)
    ).astype(BF)
    d_gates = jnp.concatenate(
        [jnp.sum(r * d_after_ffn, -1, keepdims=True) for r in expert_rows], 1)
    d_received = lax.all_to_all(d_slots, "wt", split_axis=0, concat_axis=0, tiled=True)
    d_received = d_received.reshape(W, EL, CAP, D)
    d_disp = ffn_backward(received, d_received, ffn_in, ffn_out)
    d_disp = lax.all_to_all(d_disp.reshape(slots, D), "wt", split_axis=0, concat_axis=0, tiled=True)

    x_rows = lax.all_gather(received, "seq", axis=0)
    dy_rows = lax.all_gather(d_received, "seq", axis=0)
    g_ffn_in, g_ffn_out = ffn_grads(x_rows, dy_rows, ffn_in, ffn_out)

    d_picked = gates * (d_gates - jnp.sum(gates * d_gates, -1, keepdims=True))
    d_logits = (hots[0] * d_picked[:, 0:1] + hots[1] * d_picked[:, 1:2]).astype(BF)
    g_ffn_router = dot(ffn_x, d_logits, 0, 0)
    d_ffn_x = dot(both_hot, d_disp) + dot(d_logits, small[:, C_FR:C_END], 1, 1)
    g_norm2 = jnp.sum(d_ffn_x * normed2, 0)
    d_after_attn = d_after_ffn + norm_back(d_ffn_x, normed2, spread2, gain2)

    d_all = lax.all_gather(d_after_attn.astype(BF), "seq", axis=0, tiled=True)
    dx, dg, g_q, g_kv, g_out = attn_backward(
        x_all, d_all, ids_all, gates_all, q, kv, mix, wq, wkv, wout, T, hd)
    dx = lax.all_to_all(dx, "seq", split_axis=0, concat_axis=0, tiled=True).reshape(S, T, D)
    dg = lax.psum_scatter(dg, "seq", scatter_dimension=0, tiled=True)
    a_expert = jnp.arange(EA, dtype=jnp.int32)[None]
    a_hots = [(attn_ids[:, k : k + 1] == a_expert).astype(F32) for k in range(KA)]
    a_gates = lax.dynamic_slice_in_dim(gates_all, s * T, T, 0)
    d_pick = a_gates * (dg - jnp.sum(a_gates * dg, -1, keepdims=True))
    d_alogits = sum(a_hots[k] * d_pick[:, k : k + 1] for k in range(KA)).astype(BF)
    g_attn_router = dot(attn_in, d_alogits, 0, 0)
    d_attn_in = jnp.sum(dx.astype(F32), 0) + dot(d_alogits, small[:, C_AR:C_FR], 1, 1)
    g_norm1 = jnp.sum(d_attn_in * normed1, 0)
    g_tokens = (
        (1.0 - keep) * cot + d_after_attn + norm_back(d_attn_in, normed1, spread1, gain1)
    )

    g_pack = jnp.concatenate(
        [g_norm1[:, None], g_norm2[:, None], g_halt[:, None], g_attn_router, g_ffn_router,
         jnp.zeros((D, 128 - C_END), F32)], 1)
    g_pack = lax.psum(lax.psum_scatter(g_pack, "wt", scatter_dimension=0, tiled=True), "seq")
    g_q = lax.psum_scatter(g_q, "wt", scatter_dimension=0, tiled=True)
    g_kv = lax.psum_scatter(g_kv, "wt", scatter_dimension=0, tiled=True)
    g_out = lax.all_to_all(g_out.reshape(EA, C, D), "seq", split_axis=2, concat_axis=1, tiled=True)
    g_out = lax.psum_scatter(g_out, "wt", scatter_dimension=1, tiled=True)
    g_q = lax.all_gather(g_q, "seq", axis=0).reshape(S, rows_w, EA, C)
    g_q = g_q.transpose(2, 1, 0, 3).reshape(EA, rows_w, D).astype(F32)
    g_kv = lax.all_gather(g_kv, "seq", axis=1, tiled=True).astype(F32)
    g_out = lax.all_gather(g_out, "seq", axis=2, tiled=True).astype(F32)

    return (
        block_out[None], g_tokens[None], g_pack[:, C_N1], g_pack[:, C_AR:C_FR], g_kv, g_q, g_out,
        g_pack[:, C_N2], g_pack[:, C_FR:C_END], g_ffn_in, g_ffn_out, g_pack[:, C_HALT],
    )


def solution(mesh):
    tok, exp = P("wt", "seq", None), P(None, "wt", None)
    vec, mat, ffn = P("wt"), P("wt", None), P("wt", None, None)
    return jax.shard_map(
        per_device,
        mesh=mesh,
        in_specs=(tok, P("wt", "seq"), tok, tok, vec, mat, mat, exp, exp, vec, mat, ffn, ffn, vec, tok),
        out_specs=(tok, tok, vec, mat, mat, exp, exp, vec, mat, ffn, ffn, vec),
        check_vma=False,
    )
```
